32 devices in a mesh: rep: 8 (over y, x, core), fsdp: 4 (over z).
Axes of the slice: x: 2, y: 2, z: 4, core: 2. Of those that a mesh axis runs over, the one named last changes fastest.
Arguments:
- tokens_in: bfloat16 [4096, 1024], P(('rep', 'fsdp')), may hold values from -20 to 20
- input_gain: float32 [1024], replicated, may hold values from 0.25 to 1.75
- q_gain: float32 [128], replicated, may hold values from 0.6 to 4.2
- k_gain: float32 [128], replicated, may hold values from 0.6 to 4.2
- w_query: bfloat16 [1024, 2048], P('fsdp'), may hold values from -0.35 to 0.35
- w_key: bfloat16 [1024, 1024], P('fsdp'), may hold values from -0.35 to 0.35
- w_value: bfloat16 [1024, 1024], P('fsdp'), may hold values from -0.1875 to 0.1875
- w_output: bfloat16 [2048, 1024], P('fsdp'), may hold values from -0.5 to 0.5
- post_gain: float32 [1024], replicated, may hold values from 0.25 to 1.75
- w_gate: bfloat16 [1024, 3072], P('fsdp'), may hold values from -0.1875 to 0.1875
- w_up: bfloat16 [1024, 3072], P('fsdp'), may hold values from -0.1875 to 0.1875
- w_down: bfloat16 [3072, 1024], P('fsdp'), may hold values from -0.109375 to 0.109375
- segment_ids: int32 [4096], P(('rep', 'fsdp')), may hold values from 0 to 95, as said below
- positions: int32 [4096], P(('rep', 'fsdp')), may hold values from 0 to 1926, as said below
- out_cotangent: bfloat16 [4096, 1024], P(('rep', 'fsdp')), may hold values from -19 to 19
Outputs:
- block_out: bfloat16 [4096, 1024], P(('rep', 'fsdp'))
- input_grad: bfloat16 [4096, 1024], P(('rep', 'fsdp'))
- grad_input_gain: float32 [1024], replicated
- grad_q_gain: float32 [128], replicated
- grad_k_gain: float32 [128], replicated
- grad_post_gain: float32 [1024], replicated
- grad_query: float32 [1024, 2048], P('fsdp')
- grad_key: float32 [1024, 1024], P('fsdp')
- grad_value: float32 [1024, 1024], P('fsdp')
- grad_output: float32 [2048, 1024], P('fsdp')
- grad_gate: float32 [1024, 3072], P('fsdp')
- grad_up: float32 [1024, 3072], P('fsdp')
- grad_down: float32 [3072, 1024], P('fsdp')
The draws below stay inside these ranges and needn't reach their ends.
Inputs may be any that keep to these rules, and one draw needn't show every extreme that they name: `segment_ids`: each sequence of 128 tokens holds pieces of one to three documents; ids never fall along a sequence, no two sequences share an id, and ids may skip values. `positions`: positions rise by one from a token to the next of the same document and are 0 at a document's first token; the first document of a sequence may have begun in an earlier sequence.
All inputs are finite; a program needn't handle non-finite values.
Results may differ from the reference program's by a relative error of at most 0.017.
Values may be sent and summed in bfloat16 or wider, within the bound.
A program may use at most 192 MiB of HBM per device.

```python
import math
from functools import partial
import jax
import jax.numpy as jnp
from jax import lax

D = 1024
FF = 3072
HQ = 16
KVH = 8
HD = 128
SEQ = 128
QW = 2048
KW = 1024
TOKENS = 4096


def draw_tokens_in(key, part):
    base_key = jax.random.fold_in(key, 101)
    first, second = jax.random.split(base_key)
    scales = jnp.exp(jax.random.uniform(second, (TOKENS, 1), jnp.float32, math.log(0.5), math.log(5.0)))
    base = jnp.clip(jax.random.normal(first, (TOKENS, D), jnp.float32), -4.0, 4.0)
    return (base * scales).astype(jnp.bfloat16)


def draw_out_cotangent(key, part):
    base_key = jax.random.fold_in(key, 111)
    ladder = jnp.arange(TOKENS, dtype=jnp.float32)[:, None] / max(TOKENS - 1, 1)
    ramp = 1.0 + 2.0 * ladder
    base = jnp.clip(jax.random.normal(base_key, (TOKENS, D), jnp.float32), -4.0, 4.0)
    return (base * ramp).astype(jnp.bfloat16)


def draw_q_gain(key, part):
    base_key = jax.random.fold_in(key, 301)
    return jax.random.uniform(base_key, (HD,), jnp.float32, 0.6, 1.6)


def draw_k_gain(key, part):
    base_key = jax.random.fold_in(key, 302)
    return jax.random.uniform(base_key, (HD,), jnp.float32, 0.6, 1.6)


def key_columns(key):
    base = jax.random.normal(jax.random.fold_in(key, 201), (D, KVH * HD), jnp.float32)
    return jnp.clip(base, -4.0, 4.0) * D ** (-0.5)


def draw_w_key(key, part):
    return key_columns(key).astype(jnp.bfloat16)


def draw_w_query(key, part):
    noise = jnp.clip(jax.random.normal(jax.random.fold_in(key, 202), (D, HQ * HD), jnp.float32), -4.0, 4.0) * D ** (-0.5)
    return noise.astype(jnp.bfloat16)


def document_layout(key):
    seq_count = TOKENS // SEQ
    base_key = jax.random.fold_in(key, 401)
    first, second, third = jax.random.split(base_key, 3)
    row_index = jnp.arange(seq_count, dtype=jnp.int32)[:, None]
    cuts = jax.random.randint(first, (seq_count, 2), 1, SEQ)
    present = jax.random.randint(second, (seq_count, 2), 0, 2)
    present = jnp.where(row_index == seq_count - 1, 1, jnp.where(row_index == 0, 0, present))
    cuts = jnp.where(present == 1, cuts, SEQ)
    lower = jnp.min(cuts, axis=1, keepdims=True)
    upper = jnp.max(cuts, axis=1, keepdims=True)
    offset = jax.random.randint(third, (seq_count, 1), 0, 1800)
    offset = jnp.where(row_index == 0, 1799, offset)
    ladder = jnp.arange(SEQ, dtype=jnp.int32)[None, :]
    passed = (ladder >= lower).astype(jnp.int32) + (ladder >= upper).astype(jnp.int32)
    start = jnp.where(ladder >= upper, upper, jnp.where(ladder >= lower, lower, -offset))
    seg_ids = row_index * 3 + passed
    places = ladder - start
    return (seg_ids.reshape(-1).astype(jnp.int32), places.reshape(-1).astype(jnp.int32))


def draw_segment_ids(key, part):
    return document_layout(key)[0]


def draw_positions(key, part):
    return document_layout(key)[1]


def steps_of(own_key, dims, cuts, least, top_value):
    factor_of, own = 1.0, jax.random.fold_in(own_key, 6)
    for position, blocks in cuts:
        draws = jnp.exp(jax.random.uniform(jax.random.fold_in(own, position), (blocks,), jnp.float32, least / len(cuts), top_value / len(cuts)))
        factor_of = factor_of * jnp.repeat(draws, dims[position] // blocks).reshape([-1 if axis == position else 1 for axis in range(len(dims))])
    return factor_of


def centred(key, shape, spread, bound, shards=(), kind=jnp.bfloat16):
    array = jax.random.normal(key, shape, jnp.float32) * spread
    if len(shards) > 0:
        array = steps_of(key, shape, shards, -0.22, 0.18) * array
    return jnp.clip(array, min=-bound, max=bound).astype(kind)


def setup_inputs(seed: int = 0) -> dict:
    seeds = jax.random.split(jax.random.key(seed), 16)
    tokens_in = draw_tokens_in(jax.random.fold_in(seeds[15], 71), 0)
    input_gain = jnp.clip(1.0 + 0.15 * jax.random.normal(seeds[1], (D,), jnp.float32), 0.25, 1.75)
    q_gain = draw_q_gain(jax.random.fold_in(seeds[15], 71), 0)
    k_gain = draw_k_gain(jax.random.fold_in(seeds[15], 71), 0)
    w_query = draw_w_query(jax.random.fold_in(seeds[15], 71), 0)
    w_key = draw_w_key(jax.random.fold_in(seeds[15], 71), 0)
    w_value = centred(seeds[6], (D, KW), D ** -0.5, 0.1875, ((0, 4),))
    w_output = centred(seeds[7], (QW, D), HD ** -0.5, 0.5, ((0, 4),))
    post_gain = jnp.clip(1.0 + 0.15 * jax.random.normal(seeds[8], (D,), jnp.float32), 0.25, 1.75)
    w_gate = centred(seeds[9], (D, FF), D ** -0.5, 0.1875, ((0, 4),))
    w_up = centred(seeds[10], (D, FF), D ** -0.5, 0.1875, ((0, 4),))
    w_down = centred(seeds[11], (FF, D), FF ** -0.5, 0.109375, ((0, 4),))
    segment_ids = draw_segment_ids(jax.random.fold_in(seeds[15], 71), 0)
    positions = draw_positions(jax.random.fold_in(seeds[15], 71), 0)
    out_cotangent = draw_out_cotangent(jax.random.fold_in(seeds[15], 71), 0)
    return dict(tokens_in=tokens_in, input_gain=input_gain, q_gain=q_gain, k_gain=k_gain, w_query=w_query, w_key=w_key, w_value=w_value, w_output=w_output, post_gain=post_gain, w_gate=w_gate, w_up=w_up, w_down=w_down, segment_ids=segment_ids, positions=positions, out_cotangent=out_cotangent)


EPS = 1e-06
ROPE_BASE = 1000000.0
NEG_FILL = -1e+30

def rms_scale(values):
    return lax.rsqrt(lax.optimization_barrier(jnp.mean(values * values, axis=-1, keepdims=True)) + EPS)

def rope_tables(places, width):
    halfway = width // 2
    ladder = jnp.arange(halfway, dtype=jnp.float32)
    inverse = jnp.exp(ladder * (-2.0 * math.log(ROPE_BASE) / width))
    angles = places.astype(jnp.float32)[:, None] * inverse[None, :]
    cosine = jnp.cos(angles)
    sine = jnp.sin(angles)
    return (jnp.concatenate([cosine, cosine], -1)[:, None, :], jnp.concatenate([sine, sine], -1)[:, None, :])

def rotate(values):
    halfway = values.shape[-1] // 2
    return jnp.concatenate([-values[..., halfway:], values[..., :halfway]], -1)

def apply_rope(values, cosine, sine):
    return values * cosine + rotate(values) * sine

def undo_rope(grads, cosine, sine):
    return grads * cosine - rotate(grads * sine)

def norm_back(grads, values, scale, gain):
    normal = values * scale
    gain_term = lax.optimization_barrier(jnp.sum(grads * normal, axis=tuple(range(grads.ndim - 1))))
    scaled = grads * gain
    back = scale * (scaled - normal * lax.optimization_barrier(jnp.mean(scaled * normal, axis=-1, keepdims=True)))
    return (back, gain_term)

def times_transposed(first, second):
    return lax.dot_general(first, second, (((1,), (1,)), ((), ())), preferred_element_type=jnp.float32)

def transposed_times(first, second):
    return lax.dot_general(first, second, (((0,), (0,)), ((), ())), preferred_element_type=jnp.float32)

def score_block(q_rot, k_rot, seg_ids, groups):
    length = q_rot.shape[0]
    heads_kv = k_rot.shape[1]
    width = k_rot.shape[2]
    grouped = q_rot.reshape(length, heads_kv, groups, width)
    scores = jnp.einsum('qkgd,tkd->kgqt', grouped.astype(jnp.float32), k_rot.astype(jnp.float32)) * width ** (-0.5)
    ladder = jnp.arange(length)
    allowed = (seg_ids[:, None] == seg_ids[None, :]) & (ladder[:, None] >= ladder[None, :])
    return (grouped, scores, allowed)

def attend_forward(q_rot, k_rot, values, seg_ids, groups):
    grouped, scores, allowed = score_block(q_rot, k_rot, seg_ids, groups)
    masked = jnp.where(allowed, scores, NEG_FILL)
    top = lax.optimization_barrier(jnp.max(masked, axis=-1, keepdims=True))
    log_total = top + jnp.log(lax.optimization_barrier(jnp.sum(jnp.exp(masked - top), axis=-1, keepdims=True)))
    probs = jnp.where(allowed, jnp.exp(masked - log_total), 0.0).astype(jnp.bfloat16)
    mixed = jnp.einsum('kgqt,tkd->qkgd', probs.astype(jnp.float32), values.astype(jnp.float32))
    return (mixed.reshape(q_rot.shape[0], -1).astype(jnp.bfloat16), log_total)

def attend_backward(q_rot, k_rot, values, seg_ids, log_total, d_mixed, groups):
    grouped, scores, allowed = score_block(q_rot, k_rot, seg_ids, groups)
    width = k_rot.shape[2]
    weights = jnp.where(allowed, jnp.exp(jnp.where(allowed, scores, NEG_FILL) - log_total), 0.0)
    d_grouped = d_mixed.reshape(grouped.shape)
    d_weights = jnp.einsum('qkgd,tkd->kgqt', d_grouped.astype(jnp.float32), values.astype(jnp.float32))
    centre = lax.optimization_barrier(jnp.sum(weights * d_weights, axis=-1, keepdims=True))
    d_scores = (weights * (d_weights - centre) * width ** (-0.5)).astype(jnp.bfloat16)
    d_query = jnp.einsum('kgqt,tkd->qkgd', d_scores.astype(jnp.float32), k_rot.astype(jnp.float32))
    d_key = jnp.einsum('kgqt,qkgd->tkd', d_scores.astype(jnp.float32), grouped.astype(jnp.float32))
    d_value = jnp.einsum('kgqt,qkgd->tkd', weights.astype(jnp.bfloat16).astype(jnp.float32), d_grouped.astype(jnp.float32))
    return (d_query.reshape(q_rot.shape), d_key, d_value)

def layer_forward(tokens, seg_ids, places, input_gain, q_gain, k_gain, w_query, w_key, w_value, w_output, post_gain, w_gate, w_up, w_down, seq_len):
    rows_total = tokens.shape[0]
    width = q_gain.shape[0]
    seqs = rows_total // seq_len
    heads_q = w_query.shape[1] // width
    heads_kv = w_key.shape[1] // width
    groups = heads_q // heads_kv
    tokens_float = tokens.astype(jnp.float32)
    in_scale = rms_scale(tokens_float)
    normed = (tokens_float * in_scale * input_gain).astype(jnp.bfloat16)
    queries = jnp.dot(normed, w_query, preferred_element_type=jnp.float32).reshape(rows_total, heads_q, width)
    keys = jnp.dot(normed, w_key, preferred_element_type=jnp.float32).reshape(rows_total, heads_kv, width)
    values = jnp.dot(normed, w_value, preferred_element_type=jnp.float32).astype(jnp.bfloat16).reshape(rows_total, heads_kv, width)
    cosine, sine = rope_tables(places, width)
    q_scale = rms_scale(queries)
    k_scale = rms_scale(keys)
    q_rot = apply_rope(queries * q_scale * q_gain, cosine, sine).astype(jnp.bfloat16)
    k_rot = apply_rope(keys * k_scale * k_gain, cosine, sine).astype(jnp.bfloat16)
    attend = jax.vmap(partial(attend_forward, groups=groups))
    mixed, log_total = attend(q_rot.reshape(seqs, seq_len, heads_q, width), k_rot.reshape(seqs, seq_len, heads_kv, width), values.reshape(seqs, seq_len, heads_kv, width), seg_ids.reshape(seqs, seq_len))
    attended = mixed.reshape(rows_total, heads_q * width)
    middle = tokens_float + jnp.dot(attended, w_output, preferred_element_type=jnp.float32)
    post_scale = rms_scale(middle)
    post_normed = (middle * post_scale * post_gain).astype(jnp.bfloat16)
    gate = jnp.dot(post_normed, w_gate, preferred_element_type=jnp.float32)
    up_proj = jnp.dot(post_normed, w_up, preferred_element_type=jnp.float32)
    hidden = (jax.nn.silu(gate) * up_proj).astype(jnp.bfloat16)
    block_out = (middle + jnp.dot(hidden, w_down, preferred_element_type=jnp.float32)).astype(jnp.bfloat16)
    saved = (tokens_float, in_scale, normed, queries, keys, q_scale, k_scale, values, q_rot, k_rot, cosine, sine, log_total, attended, middle, post_scale, post_normed, gate, up_proj, hidden)
    return (block_out, saved)

def layer_backward(saved, seg_ids, cotangent, input_gain, q_gain, k_gain, w_query, w_key, w_value, w_output, post_gain, w_gate, w_up, w_down, seq_len):
    tokens_float, in_scale, normed, queries, keys, q_scale, k_scale, values, q_rot, k_rot, cosine, sine, log_total, attended, middle, post_scale, post_normed, gate, up_proj, hidden = saved
    rows_total = tokens_float.shape[0]
    width = q_gain.shape[0]
    seqs = rows_total // seq_len
    heads_q = queries.shape[1]
    heads_kv = keys.shape[1]
    groups = heads_q // heads_kv
    d_hidden = times_transposed(cotangent, w_down)
    sigm = jax.nn.sigmoid(gate)
    d_gate = (d_hidden * up_proj * sigm * (1.0 + gate * (1.0 - sigm))).astype(jnp.bfloat16)
    d_up = (d_hidden * gate * sigm).astype(jnp.bfloat16)
    d_post = times_transposed(d_gate, w_gate) + times_transposed(d_up, w_up)
    d_norm_mid, post_term = norm_back(d_post, middle, post_scale, post_gain)
    d_middle = cotangent.astype(jnp.float32) + d_norm_mid
    d_attn_out = d_middle.astype(jnp.bfloat16)
    d_attended = times_transposed(d_attn_out, w_output).astype(jnp.bfloat16)
    attend_back = jax.vmap(partial(attend_backward, groups=groups))
    d_qrot, d_krot, d_vals = attend_back(q_rot.reshape(seqs, seq_len, heads_q, width), k_rot.reshape(seqs, seq_len, heads_kv, width), values.reshape(seqs, seq_len, heads_kv, width), seg_ids.reshape(seqs, seq_len), log_total, d_attended.reshape(seqs, seq_len, heads_q * width))
    q_back = undo_rope(d_qrot.reshape(rows_total, heads_q, width), cosine, sine)
    k_back = undo_rope(d_krot.reshape(rows_total, heads_kv, width), cosine, sine)
    d_q_float, q_term = norm_back(q_back, queries, q_scale, q_gain)
    d_k_float, k_term = norm_back(k_back, keys, k_scale, k_gain)
    d_queries = d_q_float.astype(jnp.bfloat16).reshape(rows_total, heads_q * width)
    d_keys = d_k_float.astype(jnp.bfloat16).reshape(rows_total, heads_kv * width)
    d_values = d_vals.astype(jnp.bfloat16).reshape(rows_total, heads_kv * width)
    d_normed = times_transposed(d_queries, w_query) + times_transposed(d_keys, w_key) + times_transposed(d_values, w_value)
    d_tokens, in_term = norm_back(d_normed, tokens_float, in_scale, input_gain)
    input_grad = (d_middle + d_tokens).astype(jnp.bfloat16)
    gains = (in_term, q_term, k_term, post_term)
    pairs = ((normed, d_queries), (normed, d_keys), (normed, d_values), (attended, d_attn_out), (post_normed, d_gate), (post_normed, d_up), (hidden, cotangent))
    return (input_grad, gains, pairs)

def reference(tokens_in, input_gain, q_gain, k_gain, w_query, w_key, w_value, w_output, post_gain, w_gate, w_up, w_down, segment_ids, positions, out_cotangent):
    seq_count = TOKENS // SEQ
    per_block = math.gcd(seq_count, max(1, 4096 // SEQ))
    block_rows = per_block * SEQ
    blocks_total = TOKENS // block_rows
    weights = (w_query, w_key, w_value, w_output, post_gain, w_gate, w_up, w_down)

    def step(carry, block):
        tokens, seg_ids, places, cotangent = block
        block_out, saved = layer_forward(tokens, seg_ids, places, input_gain, q_gain, k_gain, *weights, SEQ)
        input_grad, gains, pairs = layer_backward(saved, seg_ids, cotangent, input_gain, q_gain, k_gain, *weights, SEQ)
        grads = tuple((transposed_times(first, second) for first, second in pairs))
        updated = tuple((total + term for total, term in zip(carry, gains + grads)))
        return (updated, (block_out, input_grad))
    shapes = [(D,), (HD,), (HD,), (D,), (D, QW), (D, KW), (D, KW), (QW, D), (D, FF), (D, FF), (FF, D)]
    init = tuple((jnp.zeros(shape, jnp.float32) for shape in shapes))
    blocks = (tokens_in.reshape(blocks_total, block_rows, D), segment_ids.reshape(blocks_total, block_rows), positions.reshape(blocks_total, block_rows), out_cotangent.reshape(blocks_total, block_rows, D))
    carry, (outs, grads_in) = lax.scan(step, init, blocks)
    return (outs.reshape(TOKENS, D), grads_in.reshape(TOKENS, D), carry[0], carry[1], carry[2], carry[3], carry[4], carry[5], carry[6], carry[7], carry[8], carry[9], carry[10])
```

```python
from functools import partial
import math

import jax
import jax.numpy as jnp
from jax import lax
from jax.sharding import PartitionSpec as P

EPS = 1e-06
ROPE_BASE = 1000000.0
NEG_FILL = -1e30


def rms_scale(values):
    return lax.rsqrt(jnp.mean(values * values, axis=-1, keepdims=True) + EPS)


def rope_tables(places, width):
    halfway = width // 2
    ladder = jnp.arange(halfway, dtype=jnp.float32)
    inverse = jnp.exp(ladder * (-2.0 * math.log(ROPE_BASE) / width))
    angles = places.astype(jnp.float32)[:, None] * inverse[None, :]
    cosine = jnp.cos(angles)
    sine = jnp.sin(angles)
    return (
        jnp.concatenate([cosine, cosine], -1)[:, None, :],
        jnp.concatenate([sine, sine], -1)[:, None, :],
    )


def rotate(values):
    halfway = values.shape[-1] // 2
    return jnp.concatenate([-values[..., halfway:], values[..., :halfway]], -1)


def apply_rope(values, cosine, sine):
    return values * cosine + rotate(values) * sine


def undo_rope(grads, cosine, sine):
    return grads * cosine - rotate(grads * sine)


def norm_back(grads, values, scale, gain):
    normal = values * scale
    gain_term = jnp.sum(grads * normal, axis=tuple(range(grads.ndim - 1)))
    scaled = grads * gain
    back = scale * (scaled - normal * jnp.mean(scaled * normal, axis=-1, keepdims=True))
    return (back, gain_term)


def times_transposed(first, second):
    return lax.dot_general(
        first, second, (((1,), (1,)), ((), ())), preferred_element_type=jnp.float32
    )


def transposed_times(first, second):
    return lax.dot_general(
        first, second, (((0,), (0,)), ((), ())), preferred_element_type=jnp.float32
    )


def score_block(q_rot, k_rot, seg_ids, groups):
    length = q_rot.shape[0]
    heads_kv = k_rot.shape[1]
    width = k_rot.shape[2]
    grouped = q_rot.reshape(length, heads_kv, groups, width)
    scores = jnp.einsum(
        "qkgd,tkd->kgqt", grouped, k_rot, preferred_element_type=jnp.float32
    ) * width ** (-0.5)
    ladder = jnp.arange(length)
    allowed = (seg_ids[:, None] == seg_ids[None, :]) & (ladder[:, None] >= ladder[None, :])
    return (grouped, scores, allowed)


def attend_forward(q_rot, k_rot, values, seg_ids, groups):
    grouped, scores, allowed = score_block(q_rot, k_rot, seg_ids, groups)
    masked = jnp.where(allowed, scores, NEG_FILL)
    top = jnp.max(masked, axis=-1, keepdims=True)
    log_total = top + jnp.log(jnp.sum(jnp.exp(masked - top), axis=-1, keepdims=True))
    probs = jnp.where(allowed, jnp.exp(masked - log_total), 0.0).astype(jnp.bfloat16)
    mixed = jnp.einsum("kgqt,tkd->qkgd", probs, values, preferred_element_type=jnp.float32)
    return (mixed.reshape(q_rot.shape[0], -1).astype(jnp.bfloat16), log_total)


def attend_backward(q_rot, k_rot, values, seg_ids, log_total, d_mixed, groups):
    grouped, scores, allowed = score_block(q_rot, k_rot, seg_ids, groups)
    width = k_rot.shape[2]
    weights = jnp.where(allowed, jnp.exp(jnp.where(allowed, scores, NEG_FILL) - log_total), 0.0)
    d_grouped = d_mixed.reshape(grouped.shape)
    d_weights = jnp.einsum("qkgd,tkd->kgqt", d_grouped, values, preferred_element_type=jnp.float32)
    centre = jnp.sum(weights * d_weights, axis=-1, keepdims=True)
    d_scores = (weights * (d_weights - centre) * width ** (-0.5)).astype(jnp.bfloat16)
    d_query = jnp.einsum("kgqt,tkd->qkgd", d_scores, k_rot, preferred_element_type=jnp.float32)
    d_key = jnp.einsum("kgqt,qkgd->tkd", d_scores, grouped, preferred_element_type=jnp.float32)
    d_value = jnp.einsum(
        "kgqt,qkgd->tkd",
        weights.astype(jnp.bfloat16),
        d_grouped,
        preferred_element_type=jnp.float32,
    )
    return (d_query.reshape(q_rot.shape), d_key, d_value)


def layer_forward(
    tokens,
    seg_ids,
    places,
    input_gain,
    q_gain,
    k_gain,
    w_query,
    w_key,
    w_value,
    w_output,
    post_gain,
    w_gate,
    w_up,
    w_down,
    seq_len,
):
    rows_total = tokens.shape[0]
    width = q_gain.shape[0]
    seqs = rows_total // seq_len
    heads_q = w_query.shape[1] // width
    heads_kv = w_key.shape[1] // width
    groups = heads_q // heads_kv
    tokens_float = tokens.astype(jnp.float32)
    in_scale = rms_scale(tokens_float)
    normed = (tokens_float * in_scale * input_gain).astype(jnp.bfloat16)
    queries = jnp.dot(normed, w_query, preferred_element_type=jnp.float32).reshape(
        rows_total, heads_q, width
    )
    keys = jnp.dot(normed, w_key, preferred_element_type=jnp.float32).reshape(
        rows_total, heads_kv, width
    )
    values = (
        jnp.dot(normed, w_value, preferred_element_type=jnp.float32)
        .astype(jnp.bfloat16)
        .reshape(rows_total, heads_kv, width)
    )
    cosine, sine = rope_tables(places, width)
    q_scale = rms_scale(queries)
    k_scale = rms_scale(keys)
    q_rot = apply_rope(queries * q_scale * q_gain, cosine, sine).astype(jnp.bfloat16)
    k_rot = apply_rope(keys * k_scale * k_gain, cosine, sine).astype(jnp.bfloat16)
    attend = jax.vmap(partial(attend_forward, groups=groups))
    mixed, log_total = attend(
        q_rot.reshape(seqs, seq_len, heads_q, width),
        k_rot.reshape(seqs, seq_len, heads_kv, width),
        values.reshape(seqs, seq_len, heads_kv, width),
        seg_ids.reshape(seqs, seq_len),
    )
    attended = mixed.reshape(rows_total, heads_q * width)
    middle = tokens_float + jnp.dot(attended, w_output, preferred_element_type=jnp.float32)
    post_scale = rms_scale(middle)
    post_normed = (middle * post_scale * post_gain).astype(jnp.bfloat16)
    gate = jnp.dot(post_normed, w_gate, preferred_element_type=jnp.float32)
    up_proj = jnp.dot(post_normed, w_up, preferred_element_type=jnp.float32)
    hidden = (jax.nn.silu(gate) * up_proj).astype(jnp.bfloat16)
    block_out = (middle + jnp.dot(hidden, w_down, preferred_element_type=jnp.float32)).astype(
        jnp.bfloat16
    )
    saved = (
        tokens_float,
        in_scale,
        normed,
        queries,
        keys,
        q_scale,
        k_scale,
        values,
        q_rot,
        k_rot,
        cosine,
        sine,
        log_total,
        attended,
        middle,
        post_scale,
        post_normed,
        gate,
        up_proj,
        hidden,
    )
    return (block_out, saved)


def layer_backward(
    saved,
    seg_ids,
    cotangent,
    input_gain,
    q_gain,
    k_gain,
    w_query,
    w_key,
    w_value,
    w_output,
    post_gain,
    w_gate,
    w_up,
    w_down,
    seq_len,
):
    (
        tokens_float,
        in_scale,
        normed,
        queries,
        keys,
        q_scale,
        k_scale,
        values,
        q_rot,
        k_rot,
        cosine,
        sine,
        log_total,
        attended,
        middle,
        post_scale,
        post_normed,
        gate,
        up_proj,
        hidden,
    ) = saved
    rows_total = tokens_float.shape[0]
    width = q_gain.shape[0]
    seqs = rows_total // seq_len
    heads_q = queries.shape[1]
    heads_kv = keys.shape[1]
    groups = heads_q // heads_kv
    d_hidden = times_transposed(cotangent, w_down)
    sigm = jax.nn.sigmoid(gate)
    d_gate = (d_hidden * up_proj * sigm * (1.0 + gate * (1.0 - sigm))).astype(jnp.bfloat16)
    d_up = (d_hidden * gate * sigm).astype(jnp.bfloat16)
    d_post = times_transposed(d_gate, w_gate) + times_transposed(d_up, w_up)
    d_norm_mid, post_term = norm_back(d_post, middle, post_scale, post_gain)
    d_middle = cotangent.astype(jnp.float32) + d_norm_mid
    d_attn_out = d_middle.astype(jnp.bfloat16)
    d_attended = times_transposed(d_attn_out, w_output).astype(jnp.bfloat16)
    attend_back = jax.vmap(partial(attend_backward, groups=groups))
    d_qrot, d_krot, d_vals = attend_back(
        q_rot.reshape(seqs, seq_len, heads_q, width),
        k_rot.reshape(seqs, seq_len, heads_kv, width),
        values.reshape(seqs, seq_len, heads_kv, width),
        seg_ids.reshape(seqs, seq_len),
        log_total,
        d_attended.reshape(seqs, seq_len, heads_q * width),
    )
    q_back = undo_rope(d_qrot.reshape(rows_total, heads_q, width), cosine, sine)
    k_back = undo_rope(d_krot.reshape(rows_total, heads_kv, width), cosine, sine)
    d_q_float, q_term = norm_back(q_back, queries, q_scale, q_gain)
    d_k_float, k_term = norm_back(k_back, keys, k_scale, k_gain)
    d_queries = d_q_float.astype(jnp.bfloat16).reshape(rows_total, heads_q * width)
    d_keys = d_k_float.astype(jnp.bfloat16).reshape(rows_total, heads_kv * width)
    d_values = d_vals.astype(jnp.bfloat16).reshape(rows_total, heads_kv * width)
    d_normed = (
        times_transposed(d_queries, w_query)
        + times_transposed(d_keys, w_key)
        + times_transposed(d_values, w_value)
    )
    d_tokens, in_term = norm_back(d_normed, tokens_float, in_scale, input_gain)
    input_grad = (d_middle + d_tokens).astype(jnp.bfloat16)
    gains = (in_term, q_term, k_term, post_term)
    pairs = (
        (normed, d_queries),
        (normed, d_keys),
        (normed, d_values),
        (attended, d_attn_out),
        (post_normed, d_gate),
        (post_normed, d_up),
        (hidden, cotangent),
    )
    return (input_grad, gains, pairs)


def own_piece(shard):
    rows = shard.shape[0] // lax.axis_size("rep")
    return lax.dynamic_slice_in_dim(shard, lax.axis_index("rep") * rows, rows, 0)


def gather_whole(shard):
    return lax.all_gather(own_piece(shard), ("fsdp", "rep"), axis=0, tiled=True)


def gather_staged(shard):
    part = lax.all_gather(own_piece(shard), "fsdp", axis=0)
    full = lax.all_gather(part, "rep", axis=1)
    return full.reshape(-1, shard.shape[1])


def sum_grad(first, second):
    local = transposed_times(first, second).astype(jnp.bfloat16)
    piece = lax.psum_scatter(local, ("fsdp", "rep"), scatter_dimension=0, tiled=True)
    return lax.all_gather(piece, "rep", axis=0, tiled=True).astype(jnp.float32)


def sum_gains(gains):
    sizes = [gain.shape[0] for gain in gains]
    packed = jnp.concatenate(gains)
    total = jnp.sum(lax.all_gather(packed, ("fsdp", "rep"), axis=0), axis=0)
    cuts = [sum(sizes[:at]) for at in range(1, len(sizes))]
    return jnp.split(total, cuts)


def body(
    tokens_in,
    input_gain,
    q_gain,
    k_gain,
    w_query,
    w_key,
    w_value,
    w_output,
    post_gain,
    w_gate,
    w_up,
    w_down,
    segment_ids,
    positions,
    out_cotangent,
):
    seq_len = tokens_in.shape[0]
    attn_full = (
        gather_whole(w_query),
        gather_whole(w_key),
        gather_whole(w_value),
        gather_whole(w_output),
    )
    ffn_full = (gather_whole(w_gate), gather_staged(w_up), gather_whole(w_down))
    block_out, saved = layer_forward(
        tokens_in,
        segment_ids,
        positions,
        input_gain,
        q_gain,
        k_gain,
        attn_full[0],
        attn_full[1],
        attn_full[2],
        attn_full[3],
        post_gain,
        ffn_full[0],
        ffn_full[1],
        ffn_full[2],
        seq_len,
    )
    input_grad, gains, pairs = layer_backward(
        saved,
        segment_ids,
        out_cotangent,
        input_gain,
        q_gain,
        k_gain,
        attn_full[0],
        attn_full[1],
        attn_full[2],
        attn_full[3],
        post_gain,
        ffn_full[0],
        ffn_full[1],
        ffn_full[2],
        seq_len,
    )
    gain_total = sum_gains(gains)
    grads = tuple(sum_grad(first, second) for first, second in pairs)
    return (
        block_out,
        input_grad,
        gain_total[0],
        gain_total[1],
        gain_total[2],
        gain_total[3],
        grads[0],
        grads[1],
        grads[2],
        grads[3],
        grads[4],
        grads[5],
        grads[6],
    )


def solution(mesh):
    in_specs = (
        P(("rep", "fsdp"), None),
        P(),
        P(),
        P(),
        P("fsdp", None),
        P("fsdp", None),
        P("fsdp", None),
        P("fsdp", None),
        P(),
        P("fsdp", None),
        P("fsdp", None),
        P("fsdp", None),
        P(("rep", "fsdp")),
        P(("rep", "fsdp")),
        P(("rep", "fsdp"), None),
    )
    out_specs = (
        P(("rep", "fsdp"), None),
        P(("rep", "fsdp"), None),
        P(),
        P(),
        P(),
        P(),
        P("fsdp", None),
        P("fsdp", None),
        P("fsdp", None),
        P("fsdp", None),
        P("fsdp", None),
        P("fsdp", None),
        P("fsdp", None),
    )
    return jax.shard_map(body, mesh=mesh, in_specs=in_specs, out_specs=out_specs, check_vma=False)
```

```python
from functools import partial
import math

import jax
import jax.numpy as jnp
from jax import lax
from jax.experimental import pallas as pl
from jax.experimental.pallas import tpu as pltpu
from jax.sharding import PartitionSpec as P

EPS = 1e-06
ROPE_BASE = 1000000.0
NEG_FILL = -1e30


def rms_scale(values):
    return lax.rsqrt(jnp.mean(values * values, axis=-1, keepdims=True) + EPS)


def rope_tables(places, width):
    halfway = width // 2
    ladder = jnp.arange(halfway, dtype=jnp.float32)
    inverse = jnp.exp(ladder * (-2.0 * math.log(ROPE_BASE) / width))
    angles = places.astype(jnp.float32)[:, None] * inverse[None, :]
    cosine = jnp.cos(angles)
    sine = jnp.sin(angles)
    return (
        jnp.concatenate([cosine, cosine], -1)[:, None, :],
        jnp.concatenate([sine, sine], -1)[:, None, :],
    )


def rotate(values):
    halfway = values.shape[-1] // 2
    return jnp.concatenate([-values[..., halfway:], values[..., :halfway]], -1)


def apply_rope(values, cosine, sine):
    return values * cosine + rotate(values) * sine


def undo_rope(grads, cosine, sine):
    return grads * cosine - rotate(grads * sine)


def norm_back(grads, values, scale, gain):
    normal = values * scale
    gain_term = jnp.sum(grads * normal, axis=tuple(range(grads.ndim - 1)))
    scaled = grads * gain
    back = scale * (scaled - normal * jnp.mean(scaled * normal, axis=-1, keepdims=True))
    return (back, gain_term)


def times_transposed(first, second):
    return lax.dot_general(
        first, second, (((1,), (1,)), ((), ())), preferred_element_type=jnp.float32
    )


def transposed_times(first, second):
    return lax.dot_general(
        first, second, (((0,), (0,)), ((), ())), preferred_element_type=jnp.float32
    )


def score_block(q_rot, k_rot, seg_ids, groups):
    length = q_rot.shape[0]
    heads_kv = k_rot.shape[1]
    width = k_rot.shape[2]
    grouped = q_rot.reshape(length, heads_kv, groups, width)
    scores = jnp.einsum(
        "qkgd,tkd->kgqt", grouped, k_rot, preferred_element_type=jnp.float32
    ) * width ** (-0.5)
    ladder = jnp.arange(length)
    allowed = (seg_ids[:, None] == seg_ids[None, :]) & (ladder[:, None] >= ladder[None, :])
    return (grouped, scores, allowed)


def attend_forward(q_rot, k_rot, values, seg_ids, groups):
    grouped, scores, allowed = score_block(q_rot, k_rot, seg_ids, groups)
    masked = jnp.where(allowed, scores, NEG_FILL)
    top = jnp.max(masked, axis=-1, keepdims=True)
    log_total = top + jnp.log(jnp.sum(jnp.exp(masked - top), axis=-1, keepdims=True))
    probs = jnp.where(allowed, jnp.exp(masked - log_total), 0.0).astype(jnp.bfloat16)
    mixed = jnp.einsum("kgqt,tkd->qkgd", probs, values, preferred_element_type=jnp.float32)
    return (mixed.reshape(q_rot.shape[0], -1).astype(jnp.bfloat16), log_total)


def attend_backward(q_rot, k_rot, values, seg_ids, log_total, d_mixed, groups):
    grouped, scores, allowed = score_block(q_rot, k_rot, seg_ids, groups)
    width = k_rot.shape[2]
    weights = jnp.where(allowed, jnp.exp(jnp.where(allowed, scores, NEG_FILL) - log_total), 0.0)
    d_grouped = d_mixed.reshape(grouped.shape)
    d_weights = jnp.einsum("qkgd,tkd->kgqt", d_grouped, values, preferred_element_type=jnp.float32)
    centre = jnp.sum(weights * d_weights, axis=-1, keepdims=True)
    d_scores = (weights * (d_weights - centre) * width ** (-0.5)).astype(jnp.bfloat16)
    d_query = jnp.einsum("kgqt,tkd->qkgd", d_scores, k_rot, preferred_element_type=jnp.float32)
    d_key = jnp.einsum("kgqt,qkgd->tkd", d_scores, grouped, preferred_element_type=jnp.float32)
    d_value = jnp.einsum(
        "kgqt,qkgd->tkd",
        weights.astype(jnp.bfloat16),
        d_grouped,
        preferred_element_type=jnp.float32,
    )
    return (d_query.reshape(q_rot.shape), d_key, d_value)


def layer_forward(
    tokens,
    seg_ids,
    places,
    input_gain,
    q_gain,
    k_gain,
    w_query,
    w_key,
    w_value,
    w_output,
    post_gain,
    w_gate,
    w_up,
    w_down,
    seq_len,
):
    rows_total = tokens.shape[0]
    width = q_gain.shape[0]
    seqs = rows_total // seq_len
    heads_q = w_query.shape[1] // width
    heads_kv = w_key.shape[1] // width
    groups = heads_q // heads_kv
    tokens_float = tokens.astype(jnp.float32)
    in_scale = rms_scale(tokens_float)
    normed = (tokens_float * in_scale * input_gain).astype(jnp.bfloat16)
    queries = jnp.dot(normed, w_query, preferred_element_type=jnp.float32).reshape(
        rows_total, heads_q, width
    )
    keys = jnp.dot(normed, w_key, preferred_element_type=jnp.float32).reshape(
        rows_total, heads_kv, width
    )
    values = (
        jnp.dot(normed, w_value, preferred_element_type=jnp.float32)
        .astype(jnp.bfloat16)
        .reshape(rows_total, heads_kv, width)
    )
    cosine, sine = rope_tables(places, width)
    q_scale = rms_scale(queries)
    k_scale = rms_scale(keys)
    q_rot = apply_rope(queries * q_scale * q_gain, cosine, sine).astype(jnp.bfloat16)
    k_rot = apply_rope(keys * k_scale * k_gain, cosine, sine).astype(jnp.bfloat16)
    attend = jax.vmap(partial(attend_forward, groups=groups))
    mixed, log_total = attend(
        q_rot.reshape(seqs, seq_len, heads_q, width),
        k_rot.reshape(seqs, seq_len, heads_kv, width),
        values.reshape(seqs, seq_len, heads_kv, width),
        seg_ids.reshape(seqs, seq_len),
    )
    attended = mixed.reshape(rows_total, heads_q * width)
    middle = tokens_float + jnp.dot(attended, w_output, preferred_element_type=jnp.float32)
    post_scale = rms_scale(middle)
    post_normed = (middle * post_scale * post_gain).astype(jnp.bfloat16)
    gate = jnp.dot(post_normed, w_gate, preferred_element_type=jnp.float32)
    up_proj = jnp.dot(post_normed, w_up, preferred_element_type=jnp.float32)
    hidden = (jax.nn.silu(gate) * up_proj).astype(jnp.bfloat16)
    block_out = (middle + jnp.dot(hidden, w_down, preferred_element_type=jnp.float32)).astype(
        jnp.bfloat16
    )
    saved = (
        tokens_float,
        in_scale,
        normed,
        queries,
        keys,
        q_scale,
        k_scale,
        values,
        q_rot,
        k_rot,
        cosine,
        sine,
        log_total,
        attended,
        middle,
        post_scale,
        post_normed,
        gate,
        up_proj,
        hidden,
    )
    return (block_out, saved)


def layer_backward(
    saved,
    seg_ids,
    cotangent,
    input_gain,
    q_gain,
    k_gain,
    w_query,
    w_key,
    w_value,
    w_output,
    post_gain,
    w_gate,
    w_up,
    w_down,
    seq_len,
):
    (
        tokens_float,
        in_scale,
        normed,
        queries,
        keys,
        q_scale,
        k_scale,
        values,
        q_rot,
        k_rot,
        cosine,
        sine,
        log_total,
        attended,
        middle,
        post_scale,
        post_normed,
        gate,
        up_proj,
        hidden,
    ) = saved
    rows_total = tokens_float.shape[0]
    width = q_gain.shape[0]
    seqs = rows_total // seq_len
    heads_q = queries.shape[1]
    heads_kv = keys.shape[1]
    groups = heads_q // heads_kv
    d_hidden = times_transposed(cotangent, w_down)
    sigm = jax.nn.sigmoid(gate)
    d_gate = (d_hidden * up_proj * sigm * (1.0 + gate * (1.0 - sigm))).astype(jnp.bfloat16)
    d_up = (d_hidden * gate * sigm).astype(jnp.bfloat16)
    d_post = times_transposed(d_gate, w_gate) + times_transposed(d_up, w_up)
    d_norm_mid, post_term = norm_back(d_post, middle, post_scale, post_gain)
    d_middle = cotangent.astype(jnp.float32) + d_norm_mid
    d_attn_out = d_middle.astype(jnp.bfloat16)
    d_attended = times_transposed(d_attn_out, w_output).astype(jnp.bfloat16)
    attend_back = jax.vmap(partial(attend_backward, groups=groups))
    d_qrot, d_krot, d_vals = attend_back(
        q_rot.reshape(seqs, seq_len, heads_q, width),
        k_rot.reshape(seqs, seq_len, heads_kv, width),
        values.reshape(seqs, seq_len, heads_kv, width),
        seg_ids.reshape(seqs, seq_len),
        log_total,
        d_attended.reshape(seqs, seq_len, heads_q * width),
    )
    q_back = undo_rope(d_qrot.reshape(rows_total, heads_q, width), cosine, sine)
    k_back = undo_rope(d_krot.reshape(rows_total, heads_kv, width), cosine, sine)
    d_q_float, q_term = norm_back(q_back, queries, q_scale, q_gain)
    d_k_float, k_term = norm_back(k_back, keys, k_scale, k_gain)
    d_queries = d_q_float.astype(jnp.bfloat16).reshape(rows_total, heads_q * width)
    d_keys = d_k_float.astype(jnp.bfloat16).reshape(rows_total, heads_kv * width)
    d_values = d_vals.astype(jnp.bfloat16).reshape(rows_total, heads_kv * width)
    d_normed = (
        times_transposed(d_queries, w_query)
        + times_transposed(d_keys, w_key)
        + times_transposed(d_values, w_value)
    )
    d_tokens, in_term = norm_back(d_normed, tokens_float, in_scale, input_gain)
    input_grad = (d_middle + d_tokens).astype(jnp.bfloat16)
    gains = (in_term, q_term, k_term, post_term)
    pairs = (
        (normed, d_queries),
        (normed, d_keys),
        (normed, d_values),
        (attended, d_attn_out),
        (post_normed, d_gate),
        (post_normed, d_up),
        (hidden, cotangent),
    )
    return (input_grad, gains, pairs)


SWAPPED = (0, 1, 1, 0, 1, 0, 1)


def gather_kernel(count, groups, copies, rounds, *refs):
    shards = refs[:count]
    outs = refs[count : 2 * count]
    pieces = refs[2 * count : 3 * count]
    local_in, local_out, send_sem, recv_sem = refs[3 * count :]
    mine = lax.axis_index("rep")
    group = lax.axis_index("fsdp")

    def flip(index, bit):
        step = 1 << bit
        return index + step * (1 - 2 * (lax.rem(index // step, 2)))

    def place(rep, fsdp):
        return {"rep": rep, "fsdp": fsdp}

    barrier = pltpu.get_barrier_semaphore()
    for away in range(1, groups):
        pl.semaphore_signal(
            barrier,
            inc=1,
            device_id=place(mine, lax.rem(group + away, groups)),
            device_id_type=pl.DeviceIdType.MESH,
        )
    for bit in range(rounds):
        pl.semaphore_signal(
            barrier,
            inc=1,
            device_id=place(flip(mine, bit), group),
            device_id_type=pl.DeviceIdType.MESH,
        )
    pl.semaphore_wait(barrier, groups - 1 + rounds)

    def send(source, target, which, slot, rep, fsdp):
        copy = pltpu.make_async_remote_copy(
            src_ref=source,
            dst_ref=target,
            send_sem=send_sem.at[which, slot],
            recv_sem=recv_sem.at[which, slot],
            device_id=place(rep, fsdp),
            device_id_type=pl.DeviceIdType.MESH,
        )
        copy.start()
        return copy

    started = []
    latest = []
    for which in range(count):
        stage = []
        for away in range(1, groups):
            stage.append(
                send(
                    shards[which].at[mine],
                    outs[which].at[group, mine],
                    which,
                    away - 1,
                    mine,
                    lax.rem(group + away, groups),
                )
            )
        latest.append(stage)
        started.extend(stage)
    loads = []
    for which in range(count):
        load = pltpu.make_async_copy(shards[which].at[mine], pieces[which], local_in.at[which])
        load.start()
        loads.append(load)
    stores = []
    for which in range(count):
        loads[which].wait()
        store = pltpu.make_async_copy(
            pieces[which], outs[which].at[group, mine], local_out.at[which]
        )
        store.start()
        stores.append(store)
    held = [[mine] for _ in range(count)]
    slots = [groups - 1] * count
    orders = []
    for which in range(count):
        upper = list(range(1, rounds))
        if SWAPPED[which % len(SWAPPED)]:
            upper = upper[::-1]
        orders.append(upper + [0])
    for tick in range(count + rounds):
        for which in range(count):
            turn = tick - which
            if turn < 0 or turn > rounds:
                continue
            for copy in latest[which]:
                copy.wait_recv()
            if turn == 0:
                stores[which].wait()
            if turn == rounds:
                continue
            bit = orders[which][turn]
            stage = []
            for rep in held[which]:
                part = outs[which].at[:, rep]
                stage.append(send(part, part, which, slots[which], flip(mine, bit), group))
                slots[which] += 1
            held[which] = held[which] + [flip(rep, bit) for rep in held[which]]
            latest[which] = stage
            started.extend(stage)
    for copy in started:
        copy.wait_send()


def gather_weights(shards):
    count = len(shards)
    groups = lax.axis_size("fsdp")
    copies = lax.axis_size("rep")
    rounds = copies.bit_length() - 1
    slots = groups - 1 + copies - 1
    split = [shard.reshape(copies, -1, shard.shape[1]) for shard in shards]
    anywhere = pl.BlockSpec(memory_space=pl.ANY)
    full = pl.pallas_call(
        partial(gather_kernel, count, groups, copies, rounds),
        out_shape=[jax.ShapeDtypeStruct((groups, *part.shape), part.dtype) for part in split],
        in_specs=[anywhere] * count,
        out_specs=[anywhere] * count,
        scratch_shapes=[pltpu.VMEM(part.shape[1:], part.dtype) for part in split]
        + [
            pltpu.SemaphoreType.DMA((count,)),
            pltpu.SemaphoreType.DMA((count,)),
            pltpu.SemaphoreType.DMA((count, slots)),
            pltpu.SemaphoreType.DMA((count, slots)),
        ],
        compiler_params=pltpu.CompilerParams(collective_id=0, has_side_effects=True),
        name="gather_weights",
    )(*split)
    return [whole.reshape(-1, whole.shape[-1]) for whole in full]


def body(
    tokens_in,
    input_gain,
    q_gain,
    k_gain,
    w_query,
    w_key,
    w_value,
    w_output,
    post_gain,
    w_gate,
    w_up,
    w_down,
    segment_ids,
    positions,
    out_cotangent,
):
    seq_len = tokens_in.shape[0]
    gathered = gather_weights((w_query, w_key, w_value, w_output, w_gate, w_up, w_down))
    attn_full = tuple(gathered[:4])
    ffn_full = tuple(gathered[4:])
    block_out, saved = layer_forward(
        tokens_in,
        segment_ids,
        positions,
        input_gain,
        q_gain,
        k_gain,
        attn_full[0],
        attn_full[1],
        attn_full[2],
        attn_full[3],
        post_gain,
        ffn_full[0],
        ffn_full[1],
        ffn_full[2],
        seq_len,
    )
    input_grad, gains, pairs = layer_backward(
        saved,
        segment_ids,
        out_cotangent,
        input_gain,
        q_gain,
        k_gain,
        attn_full[0],
        attn_full[1],
        attn_full[2],
        attn_full[3],
        post_gain,
        ffn_full[0],
        ffn_full[1],
        ffn_full[2],
        seq_len,
    )
    gain_total = lax.psum((gains[0], gains[1], gains[2], gains[3]), ("rep", "fsdp"))
    lefts = (
        lax.all_to_all(pairs[0][0], "fsdp", split_axis=1, concat_axis=0, tiled=True),
        lax.all_to_all(pairs[3][0], "fsdp", split_axis=1, concat_axis=0, tiled=True),
        lax.all_to_all(pairs[4][0], "fsdp", split_axis=1, concat_axis=0, tiled=True),
        lax.all_to_all(pairs[6][0], "fsdp", split_axis=1, concat_axis=0, tiled=True),
    )
    rights = (
        lax.all_gather(pairs[0][1], "fsdp", axis=0, tiled=True),
        lax.all_gather(pairs[1][1], "fsdp", axis=0, tiled=True),
        lax.all_gather(pairs[2][1], "fsdp", axis=0, tiled=True),
        lax.all_gather(pairs[3][1], "fsdp", axis=0, tiled=True),
        lax.all_gather(pairs[4][1], "fsdp", axis=0, tiled=True),
        lax.all_gather(pairs[5][1], "fsdp", axis=0, tiled=True),
        lax.all_gather(pairs[6][1], "fsdp", axis=0, tiled=True),
    )
    owned = (
        transposed_times(lefts[0], rights[0]),
        transposed_times(lefts[0], rights[1]),
        transposed_times(lefts[0], rights[2]),
        transposed_times(lefts[1], rights[3]),
        transposed_times(lefts[2], rights[4]),
        transposed_times(lefts[2], rights[5]),
        transposed_times(lefts[3], rights[6]),
    )
    grads = (
        lax.psum(owned[0].astype(jnp.bfloat16), "rep").astype(jnp.float32),
        lax.psum(owned[1].astype(jnp.bfloat16), "rep").astype(jnp.float32),
        lax.psum(owned[2].astype(jnp.bfloat16), "rep").astype(jnp.float32),
        lax.psum(owned[3].astype(jnp.bfloat16), "rep").astype(jnp.float32),
        lax.psum(owned[4].astype(jnp.bfloat16), "rep").astype(jnp.float32),
        lax.psum(owned[5].astype(jnp.bfloat16), "rep").astype(jnp.float32),
        lax.psum(owned[6].astype(jnp.bfloat16), "rep").astype(jnp.float32),
    )
    return (
        block_out,
        input_grad,
        gain_total[0],
        gain_total[1],
        gain_total[2],
        gain_total[3],
        grads[0],
        grads[1],
        grads[2],
        grads[3],
        grads[4],
        grads[5],
        grads[6],
    )


def solution(mesh):
    in_specs = (
        P(("rep", "fsdp"), None),
        P(),
        P(),
        P(),
        P("fsdp", None),
        P("fsdp", None),
        P("fsdp", None),
        P("fsdp", None),
        P(),
        P("fsdp", None),
        P("fsdp", None),
        P("fsdp", None),
        P(("rep", "fsdp")),
        P(("rep", "fsdp")),
        P(("rep", "fsdp"), None),
    )
    out_specs = (
        P(("rep", "fsdp"), None),
        P(("rep", "fsdp"), None),
        P(),
        P(),
        P(),
        P(),
        P("fsdp", None),
        P("fsdp", None),
        P("fsdp", None),
        P("fsdp", None),
        P("fsdp", None),
        P("fsdp", None),
        P("fsdp", None),
    )
    return jax.shard_map(body, mesh=mesh, in_specs=in_specs, out_specs=out_specs, check_vma=False)
```

```python
from functools import partial
import math

import jax
import jax.numpy as jnp
from jax import lax
from jax.experimental import pallas as pl
from jax.experimental.pallas import tpu as pltpu
from jax.sharding import PartitionSpec as P

EPS = 1e-06
ROPE_BASE = 1000000.0
NEG_FILL = -1e30


def rms_scale(values):
    return lax.rsqrt(jnp.mean(values * values, axis=-1, keepdims=True) + EPS)


def rope_tables(places, width):
    halfway = width // 2
    ladder = jnp.arange(halfway, dtype=jnp.float32)
    inverse = jnp.exp(ladder * (-2.0 * math.log(ROPE_BASE) / width))
    angles = places.astype(jnp.float32)[:, None] * inverse[None, :]
    cosine = jnp.cos(angles)
    sine = jnp.sin(angles)
    return (
        jnp.concatenate([cosine, cosine], -1)[:, None, :],
        jnp.concatenate([sine, sine], -1)[:, None, :],
    )


def rotate(values):
    halfway = values.shape[-1] // 2
    return jnp.concatenate([-values[..., halfway:], values[..., :halfway]], -1)


def apply_rope(values, cosine, sine):
    return values * cosine + rotate(values) * sine


def undo_rope(grads, cosine, sine):
    return grads * cosine - rotate(grads * sine)


def norm_back(grads, values, scale, gain):
    normal = values * scale
    gain_term = jnp.sum(grads * normal, axis=tuple(range(grads.ndim - 1)))
    scaled = grads * gain
    back = scale * (scaled - normal * jnp.mean(scaled * normal, axis=-1, keepdims=True))
    return (back, gain_term)


def times_transposed(first, second):
    return lax.dot_general(
        first, second, (((1,), (1,)), ((), ())), preferred_element_type=jnp.float32
    )


def transposed_times(first, second):
    return lax.dot_general(
        first, second, (((0,), (0,)), ((), ())), preferred_element_type=jnp.float32
    )


def score_block(q_rot, k_rot, seg_ids, groups):
    length = q_rot.shape[0]
    heads_kv = k_rot.shape[1]
    width = k_rot.shape[2]
    grouped = q_rot.reshape(length, heads_kv, groups, width)
    scores = jnp.einsum(
        "qkgd,tkd->kgqt", grouped, k_rot, preferred_element_type=jnp.float32
    ) * width ** (-0.5)
    ladder = jnp.arange(length)
    allowed = (seg_ids[:, None] == seg_ids[None, :]) & (ladder[:, None] >= ladder[None, :])
    return (grouped, scores, allowed)


def attend_forward(q_rot, k_rot, values, seg_ids, groups):
    grouped, scores, allowed = score_block(q_rot, k_rot, seg_ids, groups)
    masked = jnp.where(allowed, scores, NEG_FILL)
    top = jnp.max(masked, axis=-1, keepdims=True)
    log_total = top + jnp.log(jnp.sum(jnp.exp(masked - top), axis=-1, keepdims=True))
    probs = jnp.where(allowed, jnp.exp(masked - log_total), 0.0).astype(jnp.bfloat16)
    mixed = jnp.einsum("kgqt,tkd->qkgd", probs, values, preferred_element_type=jnp.float32)
    return (mixed.reshape(q_rot.shape[0], -1).astype(jnp.bfloat16), log_total)


def attend_backward(q_rot, k_rot, values, seg_ids, log_total, d_mixed, groups):
    grouped, scores, allowed = score_block(q_rot, k_rot, seg_ids, groups)
    width = k_rot.shape[2]
    weights = jnp.where(allowed, jnp.exp(jnp.where(allowed, scores, NEG_FILL) - log_total), 0.0)
    d_grouped = d_mixed.reshape(grouped.shape)
    d_weights = jnp.einsum("qkgd,tkd->kgqt", d_grouped, values, preferred_element_type=jnp.float32)
    centre = jnp.sum(weights * d_weights, axis=-1, keepdims=True)
    d_scores = (weights * (d_weights - centre) * width ** (-0.5)).astype(jnp.bfloat16)
    d_query = jnp.einsum("kgqt,tkd->qkgd", d_scores, k_rot, preferred_element_type=jnp.float32)
    d_key = jnp.einsum("kgqt,qkgd->tkd", d_scores, grouped, preferred_element_type=jnp.float32)
    d_value = jnp.einsum(
        "kgqt,qkgd->tkd",
        weights.astype(jnp.bfloat16),
        d_grouped,
        preferred_element_type=jnp.float32,
    )
    return (d_query.reshape(q_rot.shape), d_key, d_value)


def layer_forward(
    tokens,
    seg_ids,
    places,
    input_gain,
    q_gain,
    k_gain,
    w_query,
    w_key,
    w_value,
    w_output,
    post_gain,
    w_gate,
    w_up,
    w_down,
    seq_len,
):
    rows_total = tokens.shape[0]
    width = q_gain.shape[0]
    seqs = rows_total // seq_len
    heads_q = w_query.shape[1] // width
    heads_kv = w_key.shape[1] // width
    groups = heads_q // heads_kv
    tokens_float = tokens.astype(jnp.float32)
    in_scale = rms_scale(tokens_float)
    normed = (tokens_float * in_scale * input_gain).astype(jnp.bfloat16)
    queries = jnp.dot(normed, w_query, preferred_element_type=jnp.float32).reshape(
        rows_total, heads_q, width
    )
    keys = jnp.dot(normed, w_key, preferred_element_type=jnp.float32).reshape(
        rows_total, heads_kv, width
    )
    values = (
        jnp.dot(normed, w_value, preferred_element_type=jnp.float32)
        .astype(jnp.bfloat16)
        .reshape(rows_total, heads_kv, width)
    )
    cosine, sine = rope_tables(places, width)
    q_scale = rms_scale(queries)
    k_scale = rms_scale(keys)
    q_rot = apply_rope(queries * q_scale * q_gain, cosine, sine).astype(jnp.bfloat16)
    k_rot = apply_rope(keys * k_scale * k_gain, cosine, sine).astype(jnp.bfloat16)
    attend = jax.vmap(partial(attend_forward, groups=groups))
    mixed, log_total = attend(
        q_rot.reshape(seqs, seq_len, heads_q, width),
        k_rot.reshape(seqs, seq_len, heads_kv, width),
        values.reshape(seqs, seq_len, heads_kv, width),
        seg_ids.reshape(seqs, seq_len),
    )
    attended = mixed.reshape(rows_total, heads_q * width)
    middle = tokens_float + jnp.dot(attended, w_output, preferred_element_type=jnp.float32)
    post_scale = rms_scale(middle)
    post_normed = (middle * post_scale * post_gain).astype(jnp.bfloat16)
    gate = jnp.dot(post_normed, w_gate, preferred_element_type=jnp.float32)
    up_proj = jnp.dot(post_normed, w_up, preferred_element_type=jnp.float32)
    hidden = (jax.nn.silu(gate) * up_proj).astype(jnp.bfloat16)
    block_out = (middle + jnp.dot(hidden, w_down, preferred_element_type=jnp.float32)).astype(
        jnp.bfloat16
    )
    saved = (
        tokens_float,
        in_scale,
        normed,
        queries,
        keys,
        q_scale,
        k_scale,
        values,
        q_rot,
        k_rot,
        cosine,
        sine,
        log_total,
        attended,
        middle,
        post_scale,
        post_normed,
        gate,
        up_proj,
        hidden,
    )
    return (block_out, saved)


def layer_backward(
    saved,
    seg_ids,
    cotangent,
    input_gain,
    q_gain,
    k_gain,
    w_query,
    w_key,
    w_value,
    w_output,
    post_gain,
    w_gate,
    w_up,
    w_down,
    seq_len,
):
    (
        tokens_float,
        in_scale,
        normed,
        queries,
        keys,
        q_scale,
        k_scale,
        values,
        q_rot,
        k_rot,
        cosine,
        sine,
        log_total,
        attended,
        middle,
        post_scale,
        post_normed,
        gate,
        up_proj,
        hidden,
    ) = saved
    rows_total = tokens_float.shape[0]
    width = q_gain.shape[0]
    seqs = rows_total // seq_len
    heads_q = queries.shape[1]
    heads_kv = keys.shape[1]
    groups = heads_q // heads_kv
    d_hidden = times_transposed(cotangent, w_down)
    sigm = jax.nn.sigmoid(gate)
    d_gate = (d_hidden * up_proj * sigm * (1.0 + gate * (1.0 - sigm))).astype(jnp.bfloat16)
    d_up = (d_hidden * gate * sigm).astype(jnp.bfloat16)
    d_post = times_transposed(d_gate, w_gate) + times_transposed(d_up, w_up)
    d_norm_mid, post_term = norm_back(d_post, middle, post_scale, post_gain)
    d_middle = cotangent.astype(jnp.float32) + d_norm_mid
    d_attn_out = d_middle.astype(jnp.bfloat16)
    d_attended = times_transposed(d_attn_out, w_output).astype(jnp.bfloat16)
    attend_back = jax.vmap(partial(attend_backward, groups=groups))
    d_qrot, d_krot, d_vals = attend_back(
        q_rot.reshape(seqs, seq_len, heads_q, width),
        k_rot.reshape(seqs, seq_len, heads_kv, width),
        values.reshape(seqs, seq_len, heads_kv, width),
        seg_ids.reshape(seqs, seq_len),
        log_total,
        d_attended.reshape(seqs, seq_len, heads_q * width),
    )
    q_back = undo_rope(d_qrot.reshape(rows_total, heads_q, width), cosine, sine)
    k_back = undo_rope(d_krot.reshape(rows_total, heads_kv, width), cosine, sine)
    d_q_float, q_term = norm_back(q_back, queries, q_scale, q_gain)
    d_k_float, k_term = norm_back(k_back, keys, k_scale, k_gain)
    d_queries = d_q_float.astype(jnp.bfloat16).reshape(rows_total, heads_q * width)
    d_keys = d_k_float.astype(jnp.bfloat16).reshape(rows_total, heads_kv * width)
    d_values = d_vals.astype(jnp.bfloat16).reshape(rows_total, heads_kv * width)
    d_normed = (
        times_transposed(d_queries, w_query)
        + times_transposed(d_keys, w_key)
        + times_transposed(d_values, w_value)
    )
    d_tokens, in_term = norm_back(d_normed, tokens_float, in_scale, input_gain)
    input_grad = (d_middle + d_tokens).astype(jnp.bfloat16)
    gains = (in_term, q_term, k_term, post_term)
    pairs = (
        (normed, d_queries),
        (normed, d_keys),
        (normed, d_values),
        (attended, d_attn_out),
        (post_normed, d_gate),
        (post_normed, d_up),
        (hidden, cotangent),
    )
    return (input_grad, gains, pairs)


SWAPPED = (0, 1, 1, 0, 1, 0, 1)


def gather_kernel(count, groups, copies, rounds, *refs):
    shards = refs[:count]
    outs = refs[count : 2 * count]
    pieces = refs[2 * count : 3 * count]
    local_in, local_out, send_sem, recv_sem = refs[3 * count :]
    mine = lax.axis_index("rep")
    group = lax.axis_index("fsdp")

    def flip(index, bit):
        step = 1 << bit
        return index + step * (1 - 2 * (lax.rem(index // step, 2)))

    def place(rep, fsdp):
        return {"rep": rep, "fsdp": fsdp}

    barrier = pltpu.get_barrier_semaphore()
    for away in range(1, groups):
        pl.semaphore_signal(
            barrier,
            inc=1,
            device_id=place(mine, lax.rem(group + away, groups)),
            device_id_type=pl.DeviceIdType.MESH,
        )
    for bit in range(rounds):
        pl.semaphore_signal(
            barrier,
            inc=1,
            device_id=place(flip(mine, bit), group),
            device_id_type=pl.DeviceIdType.MESH,
        )
    pl.semaphore_wait(barrier, groups - 1 + rounds)

    def send(source, target, which, slot, rep, fsdp):
        copy = pltpu.make_async_remote_copy(
            src_ref=source,
            dst_ref=target,
            send_sem=send_sem.at[which, slot],
            recv_sem=recv_sem.at[which, slot],
            device_id=place(rep, fsdp),
            device_id_type=pl.DeviceIdType.MESH,
        )
        copy.start()
        return copy

    started = []
    latest = []
    for which in range(count):
        stage = []
        for away in range(1, groups):
            stage.append(
                send(
                    shards[which].at[mine],
                    outs[which].at[group, mine],
                    which,
                    away - 1,
                    mine,
                    lax.rem(group + away, groups),
                )
            )
        latest.append(stage)
        started.extend(stage)
    loads = []
    for which in range(count):
        load = pltpu.make_async_copy(shards[which].at[mine], pieces[which], local_in.at[which])
        load.start()
        loads.append(load)
    stores = []
    for which in range(count):
        loads[which].wait()
        store = pltpu.make_async_copy(
            pieces[which], outs[which].at[group, mine], local_out.at[which]
        )
        store.start()
        stores.append(store)
    held = [[mine] for _ in range(count)]
    slots = [groups - 1] * count
    orders = []
    for which in range(count):
        upper = list(range(1, rounds))
        if SWAPPED[which % len(SWAPPED)]:
            upper = upper[::-1]
        orders.append(upper + [0])
    for tick in range(count + rounds):
        for which in range(count):
            turn = tick - which
            if turn < 0 or turn > rounds:
                continue
            for copy in latest[which]:
                copy.wait_recv()
            if turn == 0:
                stores[which].wait()
            if turn == rounds:
                continue
            bit = orders[which][turn]
            stage = []
            for rep in held[which]:
                part = outs[which].at[:, rep]
                stage.append(send(part, part, which, slots[which], flip(mine, bit), group))
                slots[which] += 1
            held[which] = held[which] + [flip(rep, bit) for rep in held[which]]
            latest[which] = stage
            started.extend(stage)
    for copy in started:
        copy.wait_send()


def gather_weights(shards):
    count = len(shards)
    groups = lax.axis_size("fsdp")
    copies = lax.axis_size("rep")
    rounds = copies.bit_length() - 1
    slots = groups - 1 + copies - 1
    split = [shard.reshape(copies, -1, shard.shape[1]) for shard in shards]
    anywhere = pl.BlockSpec(memory_space=pl.ANY)
    full = pl.pallas_call(
        partial(gather_kernel, count, groups, copies, rounds),
        out_shape=[jax.ShapeDtypeStruct((groups, *part.shape), part.dtype) for part in split],
        in_specs=[anywhere] * count,
        out_specs=[anywhere] * count,
        scratch_shapes=[pltpu.VMEM(part.shape[1:], part.dtype) for part in split]
        + [
            pltpu.SemaphoreType.DMA((count,)),
            pltpu.SemaphoreType.DMA((count,)),
            pltpu.SemaphoreType.DMA((count, slots)),
            pltpu.SemaphoreType.DMA((count, slots)),
        ],
        compiler_params=pltpu.CompilerParams(collective_id=0, has_side_effects=True),
        cost_estimate=pl.CostEstimate(
            flops=0,
            transcendentals=0,
            bytes_accessed=8 * groups * sum(2 * shard.size for shard in shards),
        ),
        name="gather_weights",
    )(*split)
    return [whole.reshape(-1, whole.shape[-1]) for whole in full]


def body(
    tokens_in,
    input_gain,
    q_gain,
    k_gain,
    w_query,
    w_key,
    w_value,
    w_output,
    post_gain,
    w_gate,
    w_up,
    w_down,
    segment_ids,
    positions,
    out_cotangent,
):
    seq_len = tokens_in.shape[0]
    gathered = gather_weights((w_query, w_key, w_value, w_output, w_gate, w_up, w_down))
    cotangent_full = lax.all_gather(out_cotangent, "fsdp", axis=0, tiled=True)
    gathered, cotangent_full = lax.optimization_barrier((gathered, cotangent_full))
    attn_full = tuple(gathered[:4])
    ffn_full = tuple(gathered[4:])
    block_out, saved = layer_forward(
        tokens_in,
        segment_ids,
        positions,
        input_gain,
        q_gain,
        k_gain,
        attn_full[0],
        attn_full[1],
        attn_full[2],
        attn_full[3],
        post_gain,
        ffn_full[0],
        ffn_full[1],
        ffn_full[2],
        seq_len,
    )
    input_grad, gains, pairs = layer_backward(
        saved,
        segment_ids,
        out_cotangent,
        input_gain,
        q_gain,
        k_gain,
        attn_full[0],
        attn_full[1],
        attn_full[2],
        attn_full[3],
        post_gain,
        ffn_full[0],
        ffn_full[1],
        ffn_full[2],
        seq_len,
    )
    gain_total = lax.psum((gains[0], gains[1], gains[2], gains[3]), ("rep", "fsdp"))
    lefts = (
        lax.all_to_all(pairs[0][0], "fsdp", split_axis=1, concat_axis=0, tiled=True),
        lax.all_to_all(pairs[3][0], "fsdp", split_axis=1, concat_axis=0, tiled=True),
        lax.all_to_all(pairs[4][0], "fsdp", split_axis=1, concat_axis=0, tiled=True),
        lax.all_to_all(pairs[6][0], "fsdp", split_axis=1, concat_axis=0, tiled=True),
    )
    early = tuple(
        lax.all_gather(pairs[at][1], "fsdp", axis=0, tiled=True) for at in (4, 5, 3)
    )
    late, early = lax.optimization_barrier((tuple(pairs[at][1] for at in range(3)), early))
    rights = tuple(lax.all_gather(part, "fsdp", axis=0, tiled=True) for part in late) + (
        early[2],
        early[0],
        early[1],
        cotangent_full,
    )
    owned = (
        transposed_times(lefts[0], rights[0]),
        transposed_times(lefts[0], rights[1]),
        transposed_times(lefts[0], rights[2]),
        transposed_times(lefts[1], rights[3]),
        transposed_times(lefts[2], rights[4]),
        transposed_times(lefts[2], rights[5]),
        transposed_times(lefts[3], rights[6]),
    )
    grads = (
        lax.psum(owned[0].astype(jnp.bfloat16), "rep").astype(jnp.float32),
        lax.psum(owned[1].astype(jnp.bfloat16), "rep").astype(jnp.float32),
        lax.psum(owned[2].astype(jnp.bfloat16), "rep").astype(jnp.float32),
        lax.psum(owned[3].astype(jnp.bfloat16), "rep").astype(jnp.float32),
        lax.psum(owned[4].astype(jnp.bfloat16), "rep").astype(jnp.float32),
        lax.psum(owned[5].astype(jnp.bfloat16), "rep").astype(jnp.float32),
        lax.psum(owned[6].astype(jnp.bfloat16), "rep").astype(jnp.float32),
    )
    return (
        block_out,
        input_grad,
        gain_total[0],
        gain_total[1],
        gain_total[2],
        gain_total[3],
        grads[0],
        grads[1],
        grads[2],
        grads[3],
        grads[4],
        grads[5],
        grads[6],
    )


def solution(mesh):
    in_specs = (
        P(("rep", "fsdp"), None),
        P(),
        P(),
        P(),
        P("fsdp", None),
        P("fsdp", None),
        P("fsdp", None),
        P("fsdp", None),
        P(),
        P("fsdp", None),
        P("fsdp", None),
        P("fsdp", None),
        P(("rep", "fsdp")),
        P(("rep", "fsdp")),
        P(("rep", "fsdp"), None),
    )
    out_specs = (
        P(("rep", "fsdp"), None),
        P(("rep", "fsdp"), None),
        P(),
        P(),
        P(),
        P(),
        P("fsdp", None),
        P("fsdp", None),
        P("fsdp", None),
        P("fsdp", None),
        P("fsdp", None),
        P("fsdp", None),
        P("fsdp", None),
    )
    return jax.shard_map(body, mesh=mesh, in_specs=in_specs, out_specs=out_specs, check_vma=False)
```
